32 devices in a mesh: dp: 4 (over z), ctx: 8 (over y, x, core).
Axes of the slice: x: 2, y: 2, z: 4, core: 2. Of those that a mesh axis runs over, the one named last changes fastest.
Arguments:
- hidden_in: bfloat16 [4, 2048, 1024], P('dp', 'ctx'), may hold values from -6 to 6
- positions: int32 [4, 2048], P('dp', 'ctx'), may hold values from 0 to 4095, as said below
- expert_ids: int32 [4, 2048, 8], P('dp', 'ctx'), may hold values from 0 to 31, all different within a row; in each aligned block of 256 rows (0 to 255, 256 to 511, ..., all dimensions but the last counted through in order) at most 80 rows name the same one
- route_weights: float32 [4, 2048, 8], P('dp', 'ctx'), may hold values from 0.03 to 0.4
- w_query: bfloat16 [1024, 1024], P(('dp', 'ctx')), may hold values from -0.75 to 0.75
- key_weight: bfloat16 [1024, 512], P(('dp', 'ctx')), may hold values from -0.75 to 0.75
- value_weight: bfloat16 [1024, 512], P(('dp', 'ctx')), may hold values from -0.1875 to 0.1875
- w_output: bfloat16 [1024, 1024], P(('dp', 'ctx')), may hold values from -0.75 to 0.75
- attn_gain: bfloat16 [1024], P(('dp', 'ctx')), may hold values from 0.099609375 to 1.8984375
- moe_gain: bfloat16 [1024], P(('dp', 'ctx')), may hold values from 0.099609375 to 1.8984375
- w_gate: bfloat16 [32, 1024, 512], P('dp'), may hold values from -0.1875 to 0.1875
- w_up: bfloat16 [32, 1024, 512], P('dp'), may hold values from -0.1875 to 0.1875
- w_down: bfloat16 [32, 512, 1024], P('dp'), may hold values from -0.5 to 0.5
- out_grad: bfloat16 [4, 2048, 1024], P('dp', 'ctx'), may hold values from -6 to 6
Outputs:
- layer_out: bfloat16 [4, 2048, 1024], P('dp', 'ctx')
- log_sums: float32 [4, 16, 2048], P('dp', None, 'ctx')
- grad_in: float32 [4, 2048, 1024], P('dp', 'ctx')
- grad_w_query: float32 [1024, 1024], P(('dp', 'ctx'))
- grad_w_key: float32 [1024, 512], P(('dp', 'ctx'))
- grad_w_value: float32 [1024, 512], P(('dp', 'ctx'))
- grad_w_output: float32 [1024, 1024], P(('dp', 'ctx'))
- grad_attn_gain: float32 [1024], P(('dp', 'ctx'))
- grad_moe_gain: float32 [1024], P(('dp', 'ctx'))
- grad_w_gate: float32 [32, 1024, 512], P('dp', 'ctx')
- grad_w_up: float32 [32, 1024, 512], P('dp', 'ctx')
- grad_w_down: float32 [32, 512, 1024], P('dp', None, 'ctx')
The draws below stay inside these ranges and needn't reach their ends.
Inputs may be any that keep to these rules, and one draw needn't show every extreme that they name: `positions`: rising along each sequence by one to three from token to token. `expert_ids`: each row names 8 different experts. Within the 256 rows of one device no expert is named more than 80 times, and that bound is reached in some device's rows.
All inputs are finite; a program needn't handle non-finite values.
Results may differ from the reference program's by a relative error of at most 0.025.
Values may be sent and summed in bfloat16 or wider, within the bound.
A program may use at most 192 MiB of HBM per device.

```python
import math
import jax
import jax.numpy as jnp
import numpy as np
from jax import lax

MODEL_DIM = 1024
QUERY_HEADS = 16
KEY_VALUE_HEADS = 8
HEAD_DIM = 64
EXPERTS = 32
TOPK = 8
FF = 512
TOK_DEV = 256
SEQ = 2048
SEQS = 4
CAP = 80
N_CTX = 8


def draw_positions(key, part):
    steps_drawn = jax.random.randint(key, (SEQS, SEQ), 0, 2).astype(jnp.int32)
    index = jnp.arange(SEQ, dtype=jnp.int32)
    steps_drawn = jnp.where(index[None, :] == 0, 0, steps_drawn)
    steps_drawn = jnp.where(index[None, :] == SEQ - 1, 1, steps_drawn)
    return (2 * index[None, :] + steps_drawn).astype(jnp.int32)


def level_of(key, dims, shards, smallest, high):
    def one(position, blocks):
        steps = jax.random.uniform(jax.random.fold_in(jax.random.fold_in(key, 6), position), (blocks,), jnp.float32, smallest / len(shards), high / len(shards))
        return jnp.repeat(jnp.exp(steps), dims[position] // blocks).reshape((-1,) + (1,) * (len(dims) - position - 1))

    factor_of = one(*shards[0])
    for cut in shards[1:]:
        factor_of = factor_of * one(*cut)
    return factor_of


def assign_block(rng, own, number, rows, amount, top, bound, skew):
    ranking = jax.random.permutation(rng, amount)
    packed, usual = portions_of(amount, rows * top, bound, skew, True), portions_of(amount, rows * top, bound, skew, False)
    places = jnp.arange(amount)

    def named(sizes, offset_by):
        used = int((sizes > 0).sum())
        fixed = max(1, used // 4)
        shifted = fixed + (places - fixed + offset_by * (used - fixed)) % max(1, amount - fixed)
        return jnp.zeros((amount,), jnp.int32).at[ranking[jnp.where(places < fixed, places, shifted)]].set(jnp.asarray(sizes, jnp.int32))

    sizes = jnp.where(number % 4 == 0, named(packed, number // 4), named(usual, number - number // 4 - 1))
    mixed = jax.random.permutation(jax.random.fold_in(own, 3), amount)
    source_of, taker = mixed[0:amount // 2 * 2:2], mixed[1:amount // 2 * 2:2]
    room = jnp.minimum(sizes[source_of] - 1, bound - sizes[taker]) // 2
    room = jnp.where((source_of == ranking[0]) | (taker == ranking[0]) | (sizes[taker] == 0), 0, jnp.maximum(room, 0))
    shifted = jax.random.randint(jax.random.fold_in(own, 4), (amount // 2,), 0, 1 << 20) % (room + 1)
    sizes = sizes.at[source_of].add(-shifted).at[taker].add(shifted)
    items = jnp.searchsorted(jnp.cumsum(sizes), jnp.arange(rows * top), side="right").astype(jnp.int32)
    table = items.reshape(top, rows).T
    table = table[jax.random.permutation(jax.random.fold_in(own, 1), rows)]
    offset_by = jax.random.randint(jax.random.fold_in(own, 2), (rows, 1), 0, top)
    return jnp.take_along_axis(table, (jnp.arange(top)[None, :] + offset_by) % top, axis=1)


def portions_of(count, total, bound, skew, full):
    weights = [(1 << 20) // math.isqrt(grade ** skew) + 1 for grade in range(1, count + 1)]
    largest = bound if full else min(bound, max(-(-total // count), total * weights[0] // sum(weights)))
    least = 1 if total - largest >= count - 1 else 0
    given, surplus = [largest] + [least] * (count - 1), total - largest - least * (count - 1)
    while surplus > 0:
        candidates = [i for i in range(1, count) if given[i] < largest] or [i for i in range(1, count) if given[i] < bound]
        pool, budget = sum([weights[i] for i in candidates]), surplus
        for i in candidates:
            extra = min(bound - given[i], max(1, budget * weights[i] // pool), surplus)
            given[i] = given[i] + extra
            surplus = surplus - extra
    return np.array(given)


def noise(own_key, shape, deviation, bound, split=(), kind=jnp.bfloat16):
    result = jax.random.normal(own_key, shape, jnp.float32) * deviation
    if len(split) > 0:
        result = level_of(own_key, shape, split, -0.22, 0.18) * result
    return jnp.clip(result, min=-bound, max=bound).astype(kind)


def setup_inputs(seed: int = 0) -> dict:
    streams_of = jax.random.split(jax.random.key(seed), 15)
    hidden_in = noise(streams_of[0], (SEQS, SEQ, MODEL_DIM), 1.0, 6.0, ((0, 4), (1, 8)))
    positions = draw_positions(jax.random.fold_in(streams_of[14], 71), 0)
    expert_ids_keys = jax.random.split(jax.random.fold_in(streams_of[2], 1), SEQS * SEQ // TOK_DEV)
    expert_ids_turns = jax.random.permutation(jax.random.fold_in(streams_of[2], 3), SEQS * SEQ // TOK_DEV)
    expert_ids = jax.vmap(lambda own, number: assign_block(jax.random.fold_in(streams_of[2], 2), own, number, TOK_DEV, EXPERTS, TOPK, CAP, 1))(expert_ids_keys, expert_ids_turns).reshape((SEQS, SEQ, TOPK))
    route_weights = jnp.clip(jnp.exp(math.log(0.4) - 2.5902672 * jax.random.uniform(streams_of[3], (SEQS, SEQ, TOPK), jnp.float32) ** level_of(streams_of[3], (SEQS, SEQ, TOPK), ((0, 4), (1, 8)), -0.2, 0.2)), 0.03, 0.4)
    w_query = noise(streams_of[4], (MODEL_DIM, QUERY_HEADS * HEAD_DIM), (MODEL_DIM // 16) ** -0.5, 0.75, ((0, 32),))
    key_weight = noise(streams_of[5], (MODEL_DIM, KEY_VALUE_HEADS * HEAD_DIM), (MODEL_DIM // 16) ** -0.5, 0.75, ((0, 32),))
    value_weight = noise(streams_of[6], (MODEL_DIM, KEY_VALUE_HEADS * HEAD_DIM), MODEL_DIM ** -0.5, 0.1875, ((0, 32),))
    w_output = noise(streams_of[7], (QUERY_HEADS * HEAD_DIM, MODEL_DIM), (MODEL_DIM // 16) ** -0.5, 0.75, ((0, 32),))
    attn_gain = jnp.clip(1.0 + 0.18 * jax.random.normal(streams_of[8], (MODEL_DIM,), jnp.float32), 0.099609375, 1.8984375).astype(jnp.bfloat16)
    moe_gain = jnp.clip(1.0 + 0.18 * jax.random.normal(streams_of[9], (MODEL_DIM,), jnp.float32), 0.099609375, 1.8984375).astype(jnp.bfloat16)
    w_gate = noise(streams_of[10], (EXPERTS, MODEL_DIM, FF), MODEL_DIM ** -0.5, 0.1875, ((0, 4),))
    w_up = noise(streams_of[11], (EXPERTS, MODEL_DIM, FF), MODEL_DIM ** -0.5, 0.1875, ((0, 4),))
    w_down = noise(streams_of[12], (EXPERTS, FF, MODEL_DIM), (FF // 4) ** -0.5, 0.5, ((0, 4),))
    out_grad = noise(streams_of[13], (SEQS, SEQ, MODEL_DIM), 1.0, 6.0, ((0, 4), (1, 8)))
    return dict(hidden_in=hidden_in, positions=positions, expert_ids=expert_ids, route_weights=route_weights, w_query=w_query, key_weight=key_weight, value_weight=value_weight, w_output=w_output, attn_gain=attn_gain, moe_gain=moe_gain, w_gate=w_gate, w_up=w_up, w_down=w_down, out_grad=out_grad)


EPSILON = 1e-06
MASKED = -1e+30

@jax.custom_vjp
def reduced_precision(v):
    return lax.optimization_barrier(v.astype(jnp.bfloat16)).astype(jnp.float32)

@jax.custom_vjp
def reduced_precision_backward(v):
    return v

def low_keep(v):
    return (reduced_precision(v), None)

def low_pass(kept, grad):
    return (grad,)

def back_keep(v):
    return (v, None)

def back_low(kept, grad):
    return (reduced_precision(grad),)
reduced_precision.defvjp(low_keep, low_pass)
reduced_precision_backward.defvjp(back_keep, back_low)

def angles_for(positions, head_size):
    half_size = head_size // 2
    inverse = jnp.exp(jnp.arange(half_size, dtype=jnp.float32) * (-2.0 * math.log(10000.0) / head_size))
    angle = positions.astype(jnp.float32)[:, None] * inverse[None, :]
    return (jnp.cos(angle)[:, None, :], jnp.sin(angle)[:, None, :])

def rotate_halves(value_rows, cosine_table, sine_table):
    half_size = value_rows.shape[-1] // 2
    leading = value_rows[..., :half_size]
    trailing = value_rows[..., half_size:]
    return jnp.concatenate([leading * cosine_table - trailing * sine_table, trailing * cosine_table + leading * sine_table], axis=-1)

def rms_norm(value_rows, gain):
    return value_rows * lax.rsqrt(lax.optimization_barrier(jnp.mean(value_rows * value_rows, axis=-1, keepdims=True)) + EPSILON) * gain

def dense_projection(left, right):
    return jnp.dot(left, right, precision=lax.Precision.HIGHEST)

def one_sequence(weights, resid, positions, expert_ids, route_weights):
    w_query, key_weight, value_weight, w_output, attn_gain, moe_gain, w_gate, w_up, w_down = weights
    sequence_length = resid.shape[0]
    repeat_factor = QUERY_HEADS // KEY_VALUE_HEADS
    score_scale = 1.0 / HEAD_DIM
    first_activation = reduced_precision(rms_norm(resid, attn_gain))
    cosine_table, sine_table = angles_for(positions, HEAD_DIM)
    query_matrix = reduced_precision(rotate_halves(reduced_precision_backward(dense_projection(first_activation, w_query)).reshape(sequence_length, QUERY_HEADS, HEAD_DIM), cosine_table, sine_table))
    query_matrix = query_matrix.reshape(sequence_length, KEY_VALUE_HEADS, repeat_factor, HEAD_DIM)
    key_rows = reduced_precision(rotate_halves(reduced_precision_backward(dense_projection(first_activation, key_weight)).reshape(sequence_length, KEY_VALUE_HEADS, HEAD_DIM), cosine_table, sine_table))
    value_rows = reduced_precision(reduced_precision_backward(dense_projection(first_activation, value_weight))).reshape(sequence_length, KEY_VALUE_HEADS, HEAD_DIM)
    block_length = math.gcd(sequence_length, 512)
    count_of_blocks = sequence_length // block_length

    def attend_causal(blocks):
        query_block, query_first = blocks
        scores = jnp.einsum('tgrd,kgd->grtk', query_block, key_rows, precision=lax.Precision.HIGHEST) * score_scale
        scores = reduced_precision_backward(scores)
        visible = jnp.arange(sequence_length, dtype=jnp.int32)[None, :] <= (query_first + jnp.arange(block_length, dtype=jnp.int32))[:, None]
        scores = jnp.where(visible, scores, MASKED)
        log_total = jax.nn.logsumexp(scores, axis=-1)
        probs = reduced_precision(jnp.exp(scores - log_total[..., None]))
        mixed = jnp.einsum('grtk,kgd->tgrd', probs, value_rows, precision=lax.Precision.HIGHEST)
        return (mixed, log_total)
    attention_values, log_normalizers = lax.map(jax.checkpoint(attend_causal), (query_matrix.reshape(count_of_blocks, block_length, KEY_VALUE_HEADS, repeat_factor, HEAD_DIM), jnp.arange(count_of_blocks, dtype=jnp.int32) * block_length))
    attn_heads = reduced_precision(reduced_precision_backward(attention_values.reshape(sequence_length, QUERY_HEADS * HEAD_DIM)))
    resid_two = resid + reduced_precision_backward(dense_projection(attn_heads, w_output))
    act_two = reduced_precision(rms_norm(resid_two, moe_gain))
    flat_ids = expert_ids.reshape(-1)
    slot_count = flat_ids.shape[0]
    order = jnp.argsort(flat_ids, stable=True).astype(jnp.int32)
    counts = lax.optimization_barrier(jnp.sum((flat_ids[:, None] == jnp.arange(EXPERTS, dtype=jnp.int32)[None, :]).astype(jnp.int32), axis=0)).astype(jnp.int32)
    starts = (jnp.cumsum(counts) - counts).astype(jnp.int32)
    most_rows = N_CTX * CAP
    flat_weights = route_weights.reshape(-1)

    def expert(blocks):
        gate_w, up_w, down_w, row_first, row_count = blocks
        offsets = jnp.arange(most_rows, dtype=jnp.int32)
        slots = order[jnp.minimum(row_first + offsets, slot_count - 1)]
        owners = (slots // TOPK).astype(jnp.int32)
        rows_in = reduced_precision_backward(act_two[owners])
        gate_pre = reduced_precision_backward(dense_projection(rows_in, gate_w))
        up_pre = reduced_precision_backward(dense_projection(rows_in, up_w))
        hidden = reduced_precision(jax.nn.silu(gate_pre) * up_pre)
        outputs = reduced_precision(reduced_precision_backward(dense_projection(hidden, down_w)))
        scaled = jnp.where(offsets < row_count, flat_weights[slots], 0.0)
        return (outputs * scaled[:, None], owners)
    contrib, owners = lax.map(jax.checkpoint(expert), (w_gate, w_up, w_down, starts, counts))
    moe_out = jnp.zeros_like(resid).at[owners.reshape(-1)].add(contrib.reshape(-1, resid.shape[1]))
    log_sums = jnp.transpose(log_normalizers, (1, 2, 0, 3)).reshape(QUERY_HEADS, sequence_length)
    return (resid_two + moe_out, log_sums)

def reference(hidden_in, positions, expert_ids, route_weights, w_query, key_weight, value_weight, w_output, attn_gain, moe_gain, w_gate, w_up, w_down, out_grad):
    floats = tuple((item.astype(jnp.float32) for item in (hidden_in, w_query, key_weight, value_weight, w_output, attn_gain, moe_gain, w_gate, w_up, w_down)))

    def forward(resid, *weights):

        def sequence_step(blocks):
            return one_sequence(weights, blocks[0], blocks[1], blocks[2], blocks[3])
        return lax.map(sequence_step, (resid, positions, expert_ids, route_weights))
    outputs, pullback, log_sums = jax.vjp(forward, *floats, has_aux=True)
    grads = pullback(out_grad.astype(jnp.float32))
    return (outputs.astype(jnp.bfloat16), log_sums, grads[0], grads[1], grads[2], grads[3], grads[4], grads[5], grads[6], grads[7], grads[8], grads[9])
```

```python
import math

import jax
import jax.numpy as jnp
from jax import lax
from jax.sharding import PartitionSpec as P

HEAD_DIM = 64
CAP = 80


EPSILON = 1e-06
MASKED = -1e30


def angles_for(positions, head_size):
    half_size = head_size // 2
    inverse = jnp.exp(
        jnp.arange(half_size, dtype=jnp.float32) * (-2.0 * math.log(10000.0) / head_size)
    )
    angle = positions.astype(jnp.float32)[:, None] * inverse[None, :]
    return (jnp.cos(angle)[:, None, :], jnp.sin(angle)[:, None, :])


def rotate_halves(value_rows, cosine_table, sine_table):
    half_size = value_rows.shape[-1] // 2
    leading = value_rows[..., :half_size]
    trailing = value_rows[..., half_size:]
    return jnp.concatenate(
        [
            leading * cosine_table - trailing * sine_table,
            trailing * cosine_table + leading * sine_table,
        ],
        axis=-1,
    )


def norm_forward(value_rows, gain):
    inverse = lax.rsqrt(jnp.mean(value_rows * value_rows, axis=-1, keepdims=True) + EPSILON)
    scaled = value_rows * inverse
    return (scaled * gain.astype(jnp.float32), scaled, inverse)


def norm_backward(upstream, scaled, inverse, gain):
    weighted = upstream * gain.astype(jnp.float32)
    inner_mean = jnp.mean(weighted * scaled, axis=-1, keepdims=True)
    return (inverse * (weighted - scaled * inner_mean), jnp.sum(upstream * scaled, axis=0))


def unchanged(carried):
    return carried


def add_rows(running, addend, row_first):
    current = lax.dynamic_slice_in_dim(running, row_first, addend.shape[0], 0)
    return lax.dynamic_update_slice_in_dim(running, current + addend, row_first, 0)


def split_blocks(shard_piece, groups, head_size):
    sequence_length = shard_piece[0].shape[0]
    block_length = math.gcd(sequence_length, 512)
    count_of_blocks = sequence_length // block_length
    blocks = (
        shard_piece[0].reshape(count_of_blocks, block_length, groups, head_size),
        shard_piece[1].reshape(count_of_blocks, block_length, groups, head_size),
        jnp.arange(count_of_blocks, dtype=jnp.int32),
    )
    return (blocks, block_length)


def attend_piece(carried, shard_piece, query_matrix, query_first, score_scale):
    groups, repeat_factor, query_rows, head_size = carried[2].shape
    blocks, block_length = split_blocks(shard_piece, groups, head_size)
    query_index = query_first + jnp.arange(query_rows, dtype=jnp.int32)

    def attend_advance(current, block):
        key_block, value_block, number = block
        key_first = number * block_length

        def attend_compute(inner):
            old_max, old_sum, old_acc = inner
            scores = (
                jnp.einsum(
                    "tgrd,kgd->grtk", query_matrix, key_block, preferred_element_type=jnp.float32
                )
                * score_scale
            )
            visible = (key_first + jnp.arange(block_length, dtype=jnp.int32))[
                None, :
            ] <= query_index[:, None]
            scores = jnp.where(visible, scores, MASKED)
            new_max = jnp.maximum(old_max, jnp.max(scores, axis=-1))
            weights = jnp.where(visible, jnp.exp(scores - new_max[..., None]), 0.0)
            factor = jnp.exp(old_max - new_max)
            new_sum = factor * old_sum + jnp.sum(weights, axis=-1)
            new_acc = factor[..., None] * old_acc + jnp.einsum(
                "grtk,kgd->grtd",
                weights.astype(jnp.bfloat16),
                value_block,
                preferred_element_type=jnp.float32,
            )
            return (new_max, new_sum, new_acc)

        current = lax.cond(key_first < query_first + query_rows, attend_compute, unchanged, current)
        return (current, None)

    result, _ = lax.scan(attend_advance, carried, blocks)
    return result


def gradient_piece(
    carried, shard_piece, query_matrix, query_first, score_scale, log_sums, heads_grad, deltas
):
    groups, repeat_factor, query_rows, head_size = carried[0].shape
    blocks, block_length = split_blocks(shard_piece, groups, head_size)
    query_index = query_first + jnp.arange(query_rows, dtype=jnp.int32)

    def gradient_advance(current, block):
        key_block, value_block, number = block
        key_first = number * block_length

        def gradient_compute(inner):
            query_part, key_total, value_total = inner
            scores = (
                jnp.einsum(
                    "tgrd,kgd->grtk", query_matrix, key_block, preferred_element_type=jnp.float32
                )
                * score_scale
            )
            visible = (key_first + jnp.arange(block_length, dtype=jnp.int32))[
                None, :
            ] <= query_index[:, None]
            scores = jnp.where(visible, scores, MASKED)
            probs = jnp.exp(scores - log_sums[..., None])
            value_part = jnp.einsum(
                "grtk,grtd->kgd",
                probs.astype(jnp.bfloat16),
                heads_grad,
                preferred_element_type=jnp.float32,
            )
            prob_grad = jnp.einsum(
                "grtd,kgd->grtk", heads_grad, value_block, preferred_element_type=jnp.float32
            )
            score_grad = (probs * (prob_grad - deltas[..., None])).astype(jnp.bfloat16)
            query_part = (
                query_part
                + jnp.einsum(
                    "grtk,kgd->grtd", score_grad, key_block, preferred_element_type=jnp.float32
                )
                * score_scale
            )
            key_part = (
                jnp.einsum(
                    "grtk,tgrd->kgd", score_grad, query_matrix, preferred_element_type=jnp.float32
                )
                * score_scale
            )
            key_total = add_rows(
                key_total, key_part.reshape(block_length, groups * head_size), key_first
            )
            value_total = add_rows(
                value_total, value_part.reshape(block_length, groups * head_size), key_first
            )
            return (query_part, key_total, value_total)

        current = lax.cond(
            key_first < query_first + query_rows, gradient_compute, unchanged, current
        )
        return (current, None)

    result, _ = lax.scan(gradient_advance, carried, blocks)
    return result


def bits_of(axis):
    count = lax.axis_size(axis)
    return [1 << number for number in range(count.bit_length() - 1)]


def swap(value, axis, bit):
    count = lax.axis_size(axis)
    return lax.ppermute(value, axis, [(index, index ^ bit) for index in range(count)])


def side_of(axis, bit):
    return (lax.axis_index(axis) // bit) % 2


def places_of(axes):
    pairs = []
    for axis in axes:
        pairs += [(axis, bit) for bit in reversed(bits_of(axis))]
    return pairs


def link_orders():
    bits = bits_of("ctx")
    return [bits[:1] + bits[1:], bits[:1] + bits[:0:-1]]


def gather_blocks(shard, pairs, order):
    held = shard
    have = []
    for pair in order:
        received = swap(held, *pair)
        place = sum(pairs.index(other) < pairs.index(pair) for other in have)
        mine = side_of(*pair)
        held = jnp.where(
            mine == 0,
            jnp.stack([held, received], axis=place),
            jnp.stack([received, held], axis=place),
        )
        have.append(pair)
    return held.reshape((-1,) + shard.shape[1:])


def scatter_blocks(blocks, lead, pairs, order):
    shape = blocks.shape
    left = blocks.reshape(shape[:lead] + (2,) * len(pairs) + shape[lead + 1 :])
    places = list(pairs)
    for pair in order:
        place = lead + places.index(pair)
        mine = side_of(*pair)
        outgoing = lax.dynamic_index_in_dim(left, 1 - mine, place, keepdims=False)
        keep = lax.dynamic_index_in_dim(left, mine, place, keepdims=False)
        received = swap(outgoing.astype(jnp.bfloat16), *pair)
        left = keep.astype(jnp.float32) + received.astype(jnp.float32)
        places.remove(pair)
        if places:
            left = left.astype(jnp.bfloat16)
    return left


def sum_everywhere(value, axes):
    for axis, bit in places_of(axes):
        value = value + swap(value, axis, bit)
    return value


def body(
    hidden_in,
    positions,
    expert_ids,
    route_weights,
    w_query,
    key_weight,
    value_weight,
    w_output,
    attn_gain,
    moe_gain,
    w_gate,
    w_up,
    w_down,
    out_grad,
):
    all_pairs = places_of(("dp", "ctx"))
    ctx_pairs = places_of(("ctx",))
    order_a, order_b = link_orders()
    spread_a, spread_b = [
        [("dp", bit) for bit in reversed(bits_of("dp"))] + [("ctx", bit) for bit in reversed(order)]
        for order in (order_a, order_b)
    ]
    narrow_a, narrow_b = [
        [("ctx", bit) for bit in order] + [("dp", bit) for bit in reversed(bits_of("dp"))]
        for order in (order_a, order_b)
    ]
    group_a, group_b = [[("ctx", bit) for bit in order] for order in (order_a, order_b)]
    query_width, key_width = w_query.shape[1], key_weight.shape[1]
    gain_block = jnp.concatenate(
        [
            attn_gain[:, None],
            moe_gain[:, None],
            jnp.zeros((attn_gain.shape[0], 126), jnp.bfloat16),
        ],
        axis=1,
    )
    first_full = gather_blocks(
        jnp.concatenate([w_query, gain_block], axis=1), all_pairs, spread_a
    )
    second_full = gather_blocks(
        jnp.concatenate([key_weight, value_weight], axis=1), all_pairs, spread_b
    )
    output_full = gather_blocks(w_output, all_pairs, spread_a)
    query_full = first_full[:, :query_width]
    gains_full = first_full[:, query_width : query_width + 2].T
    gain_one, gain_two = gains_full[0], gains_full[1]
    key_full = second_full[:, :key_width]
    value_full = second_full[:, key_width:]
    tokens_here = hidden_in.shape[1]
    model_width = hidden_in.shape[2]
    head_size = HEAD_DIM
    groups = key_weight.shape[1] // head_size
    repeat_factor = w_query.shape[1] // key_weight.shape[1]
    score_scale = 1.0 / head_size
    ctx_count = lax.axis_size("ctx")
    query_first = lax.axis_index("ctx") * tokens_here
    resid = hidden_in[0].astype(jnp.float32)
    normed_one, scaled_one, inverse_one = norm_forward(resid, gain_one)
    first_activation = normed_one.astype(jnp.bfloat16)
    cosine_table, sine_table = angles_for(positions[0], head_size)
    query_lin = jnp.dot(first_activation, query_full, preferred_element_type=jnp.float32)
    key_lin = jnp.dot(first_activation, key_full, preferred_element_type=jnp.float32)
    value_low = jnp.dot(first_activation, value_full, preferred_element_type=jnp.float32).astype(
        jnp.bfloat16
    )
    query_matrix = rotate_halves(
        query_lin.reshape(tokens_here, groups * repeat_factor, head_size), cosine_table, sine_table
    ).astype(jnp.bfloat16)
    query_matrix = query_matrix.reshape(tokens_here, groups, repeat_factor, head_size)
    keys_low = (
        rotate_halves(key_lin.reshape(tokens_here, groups, head_size), cosine_table, sine_table)
        .astype(jnp.bfloat16)
        .reshape(tokens_here, groups * head_size)
    )
    keys_all = gather_blocks(keys_low, ctx_pairs, group_a[::-1])
    values_all = gather_blocks(value_low, ctx_pairs, group_b[::-1])
    start_state = (
        jnp.full((groups, repeat_factor, tokens_here), MASKED, jnp.float32),
        jnp.zeros((groups, repeat_factor, tokens_here), jnp.float32),
        jnp.zeros((groups, repeat_factor, tokens_here, head_size), jnp.float32),
    )
    fold_state = attend_piece(
        start_state,
        (keys_all, values_all),
        query_matrix,
        query_first,
        score_scale,
    )
    run_max, run_sum, run_acc = fold_state
    log_sums = run_max + jnp.log(run_sum)
    grouped_heads = (run_acc / run_sum[..., None]).astype(jnp.bfloat16)
    attn_heads = jnp.transpose(grouped_heads, (2, 0, 1, 3)).reshape(
        tokens_here, groups * repeat_factor * head_size
    )
    resid_two = resid + jnp.dot(attn_heads, output_full, preferred_element_type=jnp.float32)
    normed_two, scaled_two, inverse_two = norm_forward(resid_two, gain_two)
    act_two = normed_two.astype(jnp.bfloat16)
    local_experts = w_gate.shape[0]
    dp_count = lax.axis_size("dp")
    expert_count = local_experts * dp_count
    hidden_width = w_gate.shape[2]
    experts_here = jnp.arange(expert_count, dtype=jnp.int32)
    named = expert_ids[0][:, :, None] == experts_here[None, None, :]
    chosen = jnp.any(named, axis=1)
    weight_table = jnp.sum(jnp.where(named, route_weights[0][:, :, None], 0.0), axis=1)
    below = jnp.tril(jnp.ones((tokens_here, tokens_here), jnp.bfloat16), -1)
    rank_table = jnp.dot(below, chosen.astype(jnp.bfloat16), preferred_element_type=jnp.float32)
    rank_table = jnp.where(chosen, rank_table, -1.0)
    tables = lax.all_gather(
        jnp.concatenate([rank_table, weight_table], axis=1), "dp", axis=0, tiled=True
    )
    grad_all = lax.all_gather(out_grad[0], "dp", axis=0, tiled=True)
    expert_first = lax.axis_index("dp") * local_experts
    ranks_mine = lax.dynamic_slice_in_dim(tables, expert_first, local_experts, 1).T
    weights_mine = lax.dynamic_slice_in_dim(
        tables, expert_count + expert_first, local_experts, 1
    ).T
    all_tokens = dp_count * tokens_here
    row_slots = dp_count * CAP
    row_number = jnp.arange(row_slots, dtype=jnp.int32)
    token_number = jnp.arange(all_tokens, dtype=jnp.int32)
    same_source = (row_number // CAP)[:, None] == (token_number // tokens_here)[None, :]
    picked = (
        (row_number % CAP).astype(jnp.float32)[None, :, None] == ranks_mine[:, None, :]
    ) & same_source[None]
    row_weights = jnp.sum(jnp.where(picked, weights_mine[:, None, :], 0.0), axis=2)
    dispatch = picked.astype(jnp.bfloat16).reshape(local_experts * row_slots, all_tokens)

    def bring(rows):
        taken = jnp.dot(dispatch, rows, preferred_element_type=jnp.float32).astype(jnp.bfloat16)
        return taken.reshape(local_experts, row_slots, model_width)

    def put_back(rows):
        summed = lax.dot_general(
            dispatch,
            rows.reshape(local_experts * row_slots, model_width),
            (((0,), (0,)), ((), ())),
            preferred_element_type=jnp.float32,
        ).astype(jnp.bfloat16)
        return lax.psum_scatter(summed, "dp", scatter_dimension=0, tiled=True).astype(jnp.float32)

    grad_out = out_grad[0].astype(jnp.float32)
    slot_grad = (row_weights[:, :, None] * bring(grad_all).astype(jnp.float32)).astype(jnp.bfloat16)
    hidden_grad = jnp.einsum("ecd,efd->ecf", slot_grad, w_down, preferred_element_type=jnp.float32)
    grouped = bring(lax.all_gather(act_two, "dp", axis=0, tiled=True))
    gate_pre = jnp.einsum("ecd,edf->ecf", grouped, w_gate, preferred_element_type=jnp.float32)
    up_pre = jnp.einsum("ecd,edf->ecf", grouped, w_up, preferred_element_type=jnp.float32)
    sigmoid_gate = jax.nn.sigmoid(gate_pre)
    hidden_low = (gate_pre * sigmoid_gate * up_pre).astype(jnp.bfloat16)
    gate_grad = (
        hidden_grad * up_pre * sigmoid_gate * (1.0 + gate_pre * (1.0 - sigmoid_gate))
    ).astype(jnp.bfloat16)
    up_grad = (hidden_grad * gate_pre * sigmoid_gate).astype(jnp.bfloat16)
    row_grad = jnp.einsum("ecf,edf->ecd", gate_grad, w_gate, preferred_element_type=jnp.float32)
    row_grad = row_grad + jnp.einsum(
        "ecf,edf->ecd", up_grad, w_up, preferred_element_type=jnp.float32
    )
    act_two_grad = put_back(row_grad.astype(jnp.bfloat16))
    expert_out = jnp.einsum(
        "ecf,efd->ecd", hidden_low, w_down, preferred_element_type=jnp.float32
    ).astype(jnp.bfloat16)
    moe_out = put_back(
        (row_weights[:, :, None] * expert_out.astype(jnp.float32)).astype(jnp.bfloat16)
    )
    layer_out = (resid_two + moe_out).astype(jnp.bfloat16)
    piece_width = model_width // ctx_count

    half_experts = local_experts // 2

    def expert_sum(left, right):
        return jnp.concatenate(
            [
                weight_one(left[:half_experts], right[:half_experts], group_a),
                weight_one(left[half_experts:], right[half_experts:], group_b),
            ],
            axis=0,
        )

    def weight_one(left, right, order):
        partial = jnp.einsum(
            "ecd,ecf->edf", left, right, preferred_element_type=jnp.float32
        ).astype(jnp.bfloat16)
        return scatter_blocks(
            partial.reshape(left.shape[0], ctx_count, piece_width, hidden_width),
            1,
            ctx_pairs,
            order,
        )

    down_sum = jnp.transpose(expert_sum(slot_grad, hidden_low), (0, 2, 1))
    gate_sum = expert_sum(grouped, gate_grad)
    up_sum = expert_sum(grouped, up_grad)
    norm_two_grad, gain_two_grad = norm_backward(act_two_grad, scaled_two, inverse_two, gain_two)
    resid_two_grad = grad_out + norm_two_grad
    resid_low = resid_two_grad.astype(jnp.bfloat16)
    output_partial = jnp.dot(attn_heads.T, resid_low, preferred_element_type=jnp.float32)
    heads_flat = jnp.dot(resid_low, output_full.T, preferred_element_type=jnp.float32).astype(
        jnp.bfloat16
    )
    heads_grad = jnp.transpose(
        heads_flat.reshape(tokens_here, groups, repeat_factor, head_size), (1, 2, 0, 3)
    )
    deltas = jnp.sum(heads_grad.astype(jnp.float32) * grouped_heads.astype(jnp.float32), axis=-1)
    seq_length = tokens_here * ctx_count
    grad_state = (
        jnp.zeros((groups, repeat_factor, tokens_here, head_size), jnp.float32),
        jnp.zeros((seq_length, groups * head_size), jnp.float32),
        jnp.zeros((seq_length, groups * head_size), jnp.float32),
    )
    back_state = gradient_piece(
        grad_state,
        (keys_all, values_all),
        query_matrix,
        query_first,
        score_scale,
        log_sums,
        heads_grad,
        deltas,
    )
    query_grad, key_total, value_total = back_state
    def rows_sum(total, order):
        return scatter_blocks(
            total.astype(jnp.bfloat16).reshape(ctx_count, tokens_here, groups * head_size),
            0,
            ctx_pairs,
            order,
        )

    key_sum = rows_sum(key_total, group_a)
    value_sum = rows_sum(value_total, group_b)
    query_rows_grad = jnp.transpose(query_grad, (2, 0, 1, 3)).reshape(
        tokens_here, groups * repeat_factor, head_size
    )
    q_lin_grad = (
        rotate_halves(query_rows_grad, cosine_table, -sine_table)
        .reshape(tokens_here, groups * repeat_factor * head_size)
        .astype(jnp.bfloat16)
    )
    k_lin_grad = (
        rotate_halves(key_sum.reshape(tokens_here, groups, head_size), cosine_table, -sine_table)
        .reshape(tokens_here, groups * head_size)
        .astype(jnp.bfloat16)
    )
    v_lin_grad = value_sum.astype(jnp.bfloat16)
    query_partial = jnp.dot(first_activation.T, q_lin_grad, preferred_element_type=jnp.float32)
    key_partial = jnp.dot(first_activation.T, k_lin_grad, preferred_element_type=jnp.float32)
    value_partial = jnp.dot(first_activation.T, v_lin_grad, preferred_element_type=jnp.float32)
    act_one_grad = jnp.dot(q_lin_grad, query_full.T, preferred_element_type=jnp.float32)
    act_one_grad = act_one_grad + jnp.dot(
        k_lin_grad, key_full.T, preferred_element_type=jnp.float32
    )
    act_one_grad = act_one_grad + jnp.dot(
        v_lin_grad, value_full.T, preferred_element_type=jnp.float32
    )
    norm_one_grad, gain_one_grad = norm_backward(act_one_grad, scaled_one, inverse_one, gain_one)
    grad_in = resid_two_grad + norm_one_grad
    device_count = dp_count * ctx_count

    def param_sum(partial, order):
        return scatter_blocks(
            partial.astype(jnp.bfloat16).reshape(
                device_count, model_width // device_count, partial.shape[1]
            ),
            0,
            all_pairs,
            order,
        )

    gain_sums = sum_everywhere(
        jnp.stack([gain_one_grad, gain_two_grad]).reshape(2, model_width // 128, 128),
        ("dp", "ctx"),
    ).reshape(2, model_width)
    gain_width = model_width // device_count
    device_number = lax.axis_index("dp") * ctx_count + lax.axis_index("ctx")
    gain_mine = lax.dynamic_slice_in_dim(gain_sums, device_number * gain_width, gain_width, 1)
    key_value_sum = param_sum(jnp.concatenate([key_partial, value_partial], axis=1), narrow_b)
    param_sums = (
        param_sum(query_partial, narrow_a),
        key_value_sum[:, :key_width],
        key_value_sum[:, key_width:],
        param_sum(output_partial, narrow_b),
        gain_mine[0],
        gain_mine[1],
    )
    expert_sums = (gate_sum, up_sum, down_sum)
    log_out = log_sums.reshape(groups * repeat_factor, tokens_here)
    return (
        layer_out[None],
        log_out[None],
        grad_in[None],
        param_sums[0],
        param_sums[1],
        param_sums[2],
        param_sums[3],
        param_sums[4],
        param_sums[5],
        expert_sums[0],
        expert_sums[1],
        expert_sums[2],
    )


def solution(mesh):
    return jax.shard_map(
        body,
        mesh=mesh,
        in_specs=(
            P("dp", "ctx", None),
            P("dp", "ctx"),
            P("dp", "ctx", None),
            P("dp", "ctx", None),
            P(("dp", "ctx"), None),
            P(("dp", "ctx"), None),
            P(("dp", "ctx"), None),
            P(("dp", "ctx"), None),
            P(("dp", "ctx")),
            P(("dp", "ctx")),
            P("dp", None, None),
            P("dp", None, None),
            P("dp", None, None),
            P("dp", "ctx", None),
        ),
        out_specs=(
            P("dp", "ctx", None),
            P("dp", None, "ctx"),
            P("dp", "ctx", None),
            P(("dp", "ctx"), None),
            P(("dp", "ctx"), None),
            P(("dp", "ctx"), None),
            P(("dp", "ctx"), None),
            P(("dp", "ctx")),
            P(("dp", "ctx")),
            P("dp", "ctx", None),
            P("dp", "ctx", None),
            P("dp", None, "ctx"),
        ),
        check_vma=False,
    )
```
